32 devices in a mesh: shot: 8 (over y, x, core), rcv: 4 (over z).
Axes of the slice: x: 2, y: 2, z: 4, core: 2. Of those that a mesh axis runs over, the one named last changes fastest.
Arguments:
- spectra: bfloat16 [4, 2, 2048, 2048], P(None, None, 'shot', 'rcv'), may hold values from -6 to 6
Outputs:
- multiples: float32 [4, 2, 2048, 2048], P('rcv', None, 'shot')
The draws below stay inside these ranges and needn't reach their ends.
All inputs are finite; a program needn't handle non-finite values.
Results may differ from the reference program's by a relative error of at most 0.0003.
Values may be sent and summed in bfloat16 or wider, within the bound.
A program may use at most 128 MiB of HBM per device.

```python
import math
import jax
import jax.numpy as jnp
from jax import lax

NG = 2048
NFREQ = 4


def block_scale(own_key, dims, split, least, largest):
    factor_of = 1.0
    for position, blocks in split:
        draws = jax.random.uniform(jax.random.fold_in(jax.random.fold_in(own_key, 6), position), (blocks,), jnp.float32, least / len(split), largest / len(split))
        factor_of = factor_of * jnp.repeat(jnp.exp(draws), dims[position] // blocks).reshape((-1,) + (1,) * (len(dims) - 1 - position))
    return factor_of


def normal_values(rng, extent, spread, bound, split=(), kind=jnp.bfloat16):
    entries = spread * jax.random.normal(rng, extent, jnp.float32)
    if split:
        entries = entries * block_scale(rng, extent, split, -0.22, 0.18)
    return jnp.clip(entries, -bound, bound).astype(kind)


def setup_inputs(seed: int = 0) -> dict:
    key_list = jax.random.split(jax.random.key(seed), 2)
    spectra = normal_values(key_list[0], (NFREQ, 2, NG, NG), 1.0, 6.0, ((2, 8), (3, 4)))
    return dict(spectra=spectra)


def one_frequency(pair):
    real_part = pair[0].astype(jnp.float32)
    imag_part = pair[1].astype(jnp.float32)
    real_out = jnp.dot(real_part, real_part, preferred_element_type=jnp.float32) - jnp.dot(imag_part, imag_part, preferred_element_type=jnp.float32)
    imag_out = jnp.dot(real_part, imag_part, preferred_element_type=jnp.float32) + jnp.dot(imag_part, real_part, preferred_element_type=jnp.float32)
    return jnp.stack([real_out, imag_out], axis=0)

def reference(spectra):
    spectral_products = lax.map(one_frequency, spectra)
    return spectral_products * (-1.0 / math.sqrt(NG))
```

```python
import functools
import math

import jax
import jax.numpy as jnp
from jax import lax
from jax.experimental import pallas as pl
from jax.experimental.pallas import tpu as pltpu
from jax.sharding import PartitionSpec as P

MESH = pl.DeviceIdType.MESH
PLANE = 8
LINE = 4

FROM_X, FROM_Y, DIAGONAL = 0, 2, 4
CORE_OWN, CORE_X, CORE_Y, CORE_DIAGONAL = 6, 8, 10, 12
KINDS = 14


def kernel(rows, cols, scale, x_ref, acc, g, own_sem, line_send, line_recv, send, recv):
    s, z = lax.axis_index("shot"), lax.axis_index("rcv")
    y, x, c = s // 4, (s // 2) % 2, s % 2
    sx = y * 4 + (1 - x) * 2 + c
    sy = (1 - y) * 4 + x * 2 + c
    sd = (1 - y) * 4 + (1 - x) * 2 + c
    sc = y * 4 + x * 2 + (1 - c)
    half = z // 2
    u = z + half * (3 - 2 * z)

    def mirrored(v):
        return v + half * (3 - 2 * v)

    order = [z, mirrored(1 - u), mirrored(2), mirrored(3)]
    others = order[1:]

    barrier = pltpu.get_barrier_semaphore()
    for peer in (sx, sy, sc):
        pl.semaphore_signal(barrier, inc=1, device_id=(peer, z), device_id_type=MESH)
    for peer in others:
        pl.semaphore_signal(barrier, inc=1, device_id=(s, peer), device_id_type=MESH)
    pl.semaphore_wait(barrier, 6)

    def block(column, part, shot):
        return g.at[part, column, pl.ds(shot * rows, rows), :]

    def along_line(peer, part):
        return pltpu.make_async_remote_copy(
            src_ref=x_ref.at[peer, part],
            dst_ref=block(z, part, s),
            send_sem=line_send.at[peer, part],
            recv_sem=line_recv.at[z, part],
            device_id=(s, peer),
            device_id_type=MESH,
        )

    def line_arrival(source, part):
        return pltpu.make_async_remote_copy(
            src_ref=x_ref.at[source, part],
            dst_ref=block(source, part, s),
            send_sem=line_send.at[source, part],
            recv_sem=line_recv.at[source, part],
            device_id=(s, source),
            device_id_type=MESH,
        )

    started = []

    def push(rnd, kind, part, shot, target, source=None):
        place = block(order[rnd], part, shot)
        copy = pltpu.make_async_remote_copy(
            src_ref=place if source is None else source,
            dst_ref=place,
            send_sem=send.at[rnd, kind + part],
            recv_sem=recv.at[rnd, kind + part],
            device_id=(target, z),
            device_id_type=MESH,
        )
        copy.start()
        started.append(copy)

    def arrive(rnd, kind, part, shot):
        place = block(order[rnd], part, shot)
        pltpu.make_async_remote_copy(
            src_ref=place,
            dst_ref=place,
            send_sem=send.at[rnd, kind + part],
            recv_sem=recv.at[rnd, kind + part],
            device_id=(sx, z),
            device_id_type=MESH,
        ).wait_recv()

    def send_relayed(rnd):
        for part, kind, target in ((0, FROM_X, sx), (1, FROM_Y, sy), (0, CORE_OWN, sc), (1, CORE_OWN, sc)):
            push(rnd, kind, part, s, target, x_ref.at[z, part] if rnd == 0 else None)

    def send_direct(rnd):
        for part, kind, target in ((1, FROM_X, sx), (0, FROM_Y, sy)):
            push(rnd, kind, part, s, target, x_ref.at[z, part] if rnd == 0 else None)

    def relay(rnd):
        arrive(rnd, FROM_X, 0, sx)
        push(rnd, DIAGONAL, 0, sx, sy)
        arrive(rnd, FROM_Y, 1, sy)
        push(rnd, DIAGONAL, 1, sy, sx)
        push(rnd, CORE_X, 0, sx, sc)
        push(rnd, CORE_Y, 1, sy, sc)

    def finish_direct(rnd):
        arrive(rnd, FROM_X, 1, sx)
        push(rnd, CORE_X, 1, sx, sc)
        arrive(rnd, FROM_Y, 0, sy)
        push(rnd, CORE_Y, 0, sy, sc)

    def finish_diagonal(rnd):
        for part in range(2):
            arrive(rnd, DIAGONAL, part, sd)
            push(rnd, CORE_DIAGONAL, part, sd, sc)

    def from_core(rnd, kind, shot):
        for part in range(2):
            arrive(rnd, kind, part, shot)

    def twin(shot):
        return shot + 1 - 2 * c

    def drain(rnd):
        from_core(rnd, CORE_OWN, sc)
        from_core(rnd, CORE_X, twin(sx))
        from_core(rnd, CORE_Y, twin(sy))
        from_core(rnd, CORE_DIAGONAL, twin(sd))

    tile = 512

    def chip_product(column, chip, lanes):
        left = [g[part, chip, pl.ds(s * rows, rows), :] for part in range(2)]
        deep = pl.ds(chip * cols, cols)
        right = [g[part, column, deep, lanes] for part in range(2)]
        dot = functools.partial(jnp.dot, preferred_element_type=jnp.float32)
        real = dot(left[0], right[0]) - dot(left[1], right[1])
        imag = dot(left[0], right[1]) + dot(left[1], right[0])
        return real, imag

    def multiply(rnd, chips, first, last):
        column = order[rnd]

        @pl.loop(0, cols // tile)
        def _(t):
            lanes = pl.ds(pl.multiple_of(t * tile, tile), tile)
            wide = pl.ds(pl.multiple_of(column * cols + t * tile, tile), tile)
            real = imag = None
            for chip in chips:
                a, b = chip_product(column, chip, lanes)
                real = a if real is None else real + a
                imag = b if imag is None else imag + b
            if not first:
                real = real + acc[0, :, wide]
                imag = imag + acc[1, :, wide]
            acc[0, :, wide] = real * scale if last else real
            acc[1, :, wide] = imag * scale if last else imag

    def multiply_part(part, chip, last, first=0, deep=cols):
        column = order[-1]

        @pl.loop(0, cols // tile)
        def _(t):
            lanes = pl.ds(pl.multiple_of(t * tile, tile), tile)
            wide = pl.ds(pl.multiple_of(column * cols + t * tile, tile), tile)
            if deep == cols:
                left = [g[p, chip, pl.ds(s * rows, rows), :] for p in range(2)]
            else:
                span = pl.ds(pl.multiple_of(first, rows), rows)
                left = [g[p, chip, pl.ds(s * rows, rows), span] for p in range(2)]
            right = g[part, column, pl.ds(chip * cols + first, deep), lanes]
            dot = functools.partial(jnp.dot, preferred_element_type=jnp.float32)
            a, b = dot(left[part], right), dot(left[1 - part], right)
            real = acc[0, :, wide] + (a if part == 0 else -a)
            imag = acc[1, :, wide] + b
            acc[0, :, wide] = real * scale if last else real
            acc[1, :, wide] = imag * scale if last else imag

    def multiply_shot(part, shot, last):
        multiply_part(part, shot // 2, last, (shot % 2) * rows, rows)

    every = range(LINE)

    own = pltpu.make_async_copy(x_ref.at[z], g.at[:, z, pl.ds(s * rows, rows), :], own_sem)

    def toward(peer, begin):
        for part in range(2):
            copy = along_line(peer, part)
            copy.start() if begin else copy.wait_send()

    send_relayed(0)
    toward(others[0], True)
    own.start()
    send_direct(0)

    @pl.when(u == 1)
    def _():
        toward(others[1], True)

    own.wait()
    relay(0)

    @pl.when(u == 1)
    def _():
        toward(others[1], False)
        toward(others[2], True)

    for rnd in range(1, LINE):
        for part in range(2):
            line_arrival(order[rnd], part).wait_recv()
        send_relayed(rnd)
        finish_direct(rnd - 1)
        if rnd == LINE - 1:
            drain(0)
            multiply(0, every, True, True)
        finish_diagonal(rnd - 1)
        send_direct(rnd)
        if rnd < LINE - 1:

            @pl.when(u == 0)
            def _(peer=others[rnd]):
                toward(peer, True)

        if rnd == LINE - 1:
            drain(1)
            multiply(1, every, True, True)
        relay(rnd)
    last = LINE - 1
    drain(last - 1)
    multiply(last - 1, every, True, True)
    from_core(last, CORE_OWN, sc)
    multiply(last, [s // 2], True, False)
    finish_direct(last)
    arrive(last, CORE_X, 0, twin(sx))
    multiply_part(0, sx // 2, False)
    arrive(last, CORE_Y, 1, twin(sy))
    multiply_part(1, sy // 2, False)
    arrive(last, CORE_X, 1, twin(sx))
    multiply_part(1, sx // 2, False)
    arrive(last, CORE_Y, 0, twin(sy))
    multiply_part(0, sy // 2, False)
    finish_diagonal(last)
    for part in range(2):
        multiply_shot(part, sd, False)
    for part in range(2):
        arrive(last, CORE_DIAGONAL, part, twin(sd))
        multiply_shot(part, twin(sd), part == 1)
    for copy in started:
        copy.wait_send()
    toward(others[0], False)
    toward(others[2], False)

    @pl.when(u == 0)
    def _():
        toward(others[1], False)


def in_one_kernel(spectra):
    freqs, parts, rows, cols = spectra.shape
    full = cols * LINE
    return pl.pallas_call(
        functools.partial(kernel, rows, cols, -1.0 / math.sqrt(full)),
        out_shape=pltpu.VMEM((parts, rows, full), jnp.float32),
        in_specs=[pl.BlockSpec(memory_space=pltpu.HBM)],
        out_specs=pl.BlockSpec(memory_space=pltpu.VMEM),
        scratch_shapes=[
            pltpu.VMEM((parts, LINE, rows * PLANE, cols), jnp.bfloat16),
            pltpu.SemaphoreType.DMA,
            pltpu.SemaphoreType.DMA((LINE, 2)),
            pltpu.SemaphoreType.DMA((LINE, 2)),
            pltpu.SemaphoreType.DMA((LINE, KINDS)),
            pltpu.SemaphoreType.DMA((LINE, KINDS)),
        ],
        compiler_params=pltpu.CompilerParams(
            collective_id=0, has_side_effects=True, vmem_limit_bytes=28 * 2**20
        ),
    )(pltpu.with_memory_space_constraint(spectra, pltpu.HBM))[None]


def by_collectives(spectra):
    own_rows = lax.all_to_all(spectra, "rcv", split_axis=0, concat_axis=3, tiled=True)
    full = own_rows.shape[3]
    gathered = lax.all_gather(own_rows, "shot", axis=2, tiled=True)
    dot = functools.partial(jnp.einsum, "ang,agv->anv", preferred_element_type=jnp.float32)
    real = dot(own_rows[:, 0], gathered[:, 0]) - dot(own_rows[:, 1], gathered[:, 1])
    imag = dot(own_rows[:, 0], gathered[:, 1]) + dot(own_rows[:, 1], gathered[:, 0])
    return jnp.stack([real, imag], axis=1) * (-1.0 / math.sqrt(full))


def solution(mesh):
    fits = mesh.shape["shot"] == PLANE and mesh.shape["rcv"] == LINE
    return jax.shard_map(
        in_one_kernel if fits else by_collectives,
        mesh=mesh,
        in_specs=(P(None, None, "shot", "rcv"),),
        out_specs=P("rcv", None, "shot", None),
        check_vma=False,
    )
```

```python
import functools
import math

import jax
import jax.numpy as jnp
from jax import lax
from jax.experimental import pallas as pl
from jax.experimental.pallas import tpu as pltpu
from jax.sharding import PartitionSpec as P

MESH = pl.DeviceIdType.MESH
PLANE = 8
LINE = 4
QUARTERS = range(4)

FROM_X, FROM_Y, DIAGONAL = 0, 2, 4
CORE_OWN, CORE_X, CORE_Y, CORE_DIAGONAL = 6, 8, 10, 12
STRIP_Y, CORE_STRIP, CORE_STRIP_Y, SUMS = 14, 18, 22, 26
KINDS = 30

POWER_RANGE = 181.0
LEAST = 1e-36


def kernel(rows, cols, scale, x_ref, acc, g, coded_out, coded_in, own_sem, line_send, line_recv, send, recv):
    s, z = lax.axis_index("shot"), lax.axis_index("rcv")
    y, x, c = s // 4, (s // 2) % 2, s % 2
    sx = y * 4 + (1 - x) * 2 + c
    sy = (1 - y) * 4 + x * 2 + c
    sd = (1 - y) * 4 + (1 - x) * 2 + c
    sc = y * 4 + x * 2 + (1 - c)
    near, across, far = z + 1 - 2 * (z % 2), (z + 2) % 4, 3 - z
    early = (z + x) % 2
    inner = ((z + 1) // 2) % 2
    third = far + early * (across - far)
    fourth = across + early * (far - across)
    order = [z, near, third, fourth]
    theirs = [z, near, fourth, third]
    strip = cols // 4

    own = pltpu.make_async_copy(x_ref.at[z], g.at[:, z, pl.ds(s * rows, rows), :], own_sem)
    own.start()

    barrier = pltpu.get_barrier_semaphore()
    for peer in (sx, sy, sc):
        pl.semaphore_signal(barrier, inc=1, device_id=(peer, z), device_id_type=MESH)
    for peer in (near, across, far):
        pl.semaphore_signal(barrier, inc=1, device_id=(s, peer), device_id_type=MESH)
    pl.semaphore_wait(barrier, 6)

    def block(column, part, shot):
        return g.at[part, column, pl.ds(shot * rows, rows), :]

    def narrow(column, q, shot):
        return g.at[:, column, pl.ds(shot * rows, rows), pl.ds(q * strip, strip)]

    def line(dest, source, i, by_strips):
        if by_strips:
            src, dst = x_ref.at[dest, :, :, pl.ds(i * strip, strip)], narrow(source, i, s)
        else:
            src, dst = x_ref.at[dest, i], block(source, i, s)
        return pltpu.make_async_remote_copy(
            src_ref=src,
            dst_ref=dst,
            send_sem=line_send.at[dest, i],
            recv_sem=line_recv.at[source, i],
            device_id=(s, dest),
            device_id_type=MESH,
        )

    def toward(peer, begin, by_strips):
        for i in range(4 if by_strips else 2):
            copy = line(peer, z, i, by_strips)
            copy.start() if begin else copy.wait_send()

    def copy(rnd, kind, ref, target):
        return pltpu.make_async_remote_copy(
            src_ref=ref,
            dst_ref=ref,
            send_sem=send.at[rnd, kind],
            recv_sem=recv.at[rnd, kind],
            device_id=(target, z),
            device_id_type=MESH,
        )

    started = []

    def push(rnd, kind, part, shot, target, columns=order):
        started.append(copy(rnd, kind + part, block(columns[rnd], part, shot), target))
        started[-1].start()

    def arrive(rnd, kind, part, shot, columns=order):
        copy(rnd, kind + part, block(columns[rnd], part, shot), sx).wait_recv()

    def push_strip(kind, q, shot, target):
        started.append(copy(3, kind + q, narrow(fourth, q, shot), target))
        started[-1].start()

    def strip_arrived(kind, q, shot):
        copy(3, kind + q, narrow(fourth, q, shot), sx).wait_recv()

    def send_relayed(rnd):
        for part, kind, target in ((0, FROM_X, sx), (1, FROM_Y, sy), (0, CORE_OWN, sc), (1, CORE_OWN, sc)):
            push(rnd, kind, part, s, target)

    def send_direct(rnd):
        for part, kind, target in ((1, FROM_X, sx), (0, FROM_Y, sy)):
            push(rnd, kind, part, s, target)

    def relay(rnd):
        arrive(rnd, FROM_X, 0, sx)
        push(rnd, DIAGONAL, 0, sx, sy)
        arrive(rnd, FROM_Y, 1, sy)
        push(rnd, DIAGONAL, 1, sy, sx)
        push(rnd, CORE_X, 0, sx, sc)
        push(rnd, CORE_Y, 1, sy, sc)

    def finish_direct(rnd):
        arrive(rnd, FROM_X, 1, sx)
        push(rnd, CORE_X, 1, sx, sc)
        arrive(rnd, FROM_Y, 0, sy)
        push(rnd, CORE_Y, 0, sy, sc)

    def finish_diagonal(rnd, columns=order):
        for part in range(2):
            arrive(rnd, DIAGONAL, part, sd, columns)
            push(rnd, CORE_DIAGONAL, part, sd, sc, columns)

    def from_core(rnd, kind, shot, columns=order):
        for part in range(2):
            arrive(rnd, kind, part, shot, columns)

    def twin(shot):
        return shot + 1 - 2 * c

    def drain(rnd):
        from_core(rnd, CORE_OWN, sc)
        from_core(rnd, CORE_X, twin(sx))
        from_core(rnd, CORE_Y, twin(sy))
        from_core(rnd, CORE_DIAGONAL, twin(sd))

    tile = 512

    def product(shot, column, chips, lanes):
        real = imag = None
        dot = functools.partial(jnp.dot, preferred_element_type=jnp.float32)
        for chip in chips:
            left = [g[part, chip, pl.ds(shot * rows, rows), :] for part in range(2)]
            deep = pl.ds(pl.multiple_of(chip * cols, cols), cols)
            right = [g[part, column, deep, lanes] for part in range(2)]
            a = dot(left[0], right[0]) - dot(left[1], right[1])
            b = dot(left[0], right[1]) + dot(left[1], right[0])
            real = a if real is None else real + a
            imag = b if imag is None else imag + b
        return real, imag

    def multiply(column, chips, first):
        @pl.loop(0, cols // tile)
        def _(t):
            lanes = pl.ds(pl.multiple_of(t * tile, tile), tile)
            wide = pl.ds(pl.multiple_of(column * cols + t * tile, tile), tile)
            sums = product(s, column, chips, lanes)
            for part in range(2):
                value = sums[part] * scale
                acc[part, :, wide] = value if first else acc[part, :, wide] + value

    every = range(LINE)
    mine = [s // 2, sy // 2]

    def sums_copy(q):
        return pltpu.make_async_remote_copy(
            src_ref=coded_out.at[q],
            dst_ref=coded_in.at[q],
            send_sem=send.at[3, SUMS + q],
            recv_sem=recv.at[3, SUMS + q],
            device_id=(sx, z),
            device_id_type=MESH,
        )

    def encode(q):
        parts = product(sx, fourth, mine, pl.ds(q * strip, strip))
        largest = jnp.maximum(jnp.max(jnp.abs(parts[0])), jnp.max(jnp.abs(parts[1])))
        unit = jnp.full((16, strip), jnp.maximum(largest * 1.01, LEAST), jnp.float32).astype(jnp.bfloat16)
        coded_out[q, pl.ds(2 * rows, 16), :] = unit
        factor = POWER_RANGE / unit.astype(jnp.float32)[0:1, :]
        for p in range(2):
            v = parts[p] * factor
            w = v * v
            w = w * w
            w = w * w
            w = w * w
            coded_out[q, pl.ds(p * rows, rows), :] = jnp.where(v < 0, -w, w).astype(jnp.bfloat16)
        sums_copy(q).start()

    def decode(q):
        sums_copy(q).wait_recv()
        lanes = pl.ds(pl.multiple_of(third * cols + q * strip, strip), strip)
        unit = coded_in[q, pl.ds(2 * rows, 16), :].astype(jnp.float32)[0:1, :]
        factor = unit * (scale / POWER_RANGE)
        for p in range(2):
            w = coded_in[q, pl.ds(p * rows, rows), :].astype(jnp.float32)
            root = jnp.exp(jnp.log(jnp.abs(w)) * 0.0625)
            v = jnp.where(w == 0, 0.0, jnp.where(w < 0, -root, root))
            acc[p, :, lanes] = acc[p, :, lanes] + v * factor

    own.wait()
    send_relayed(0)
    toward(near, True, False)

    @pl.when(early * inner == 1)
    def _():
        toward(far, True, False)
        toward(across, True, False)

    @pl.when(early * (1 - inner) == 1)
    def _():
        toward(across, True, False)
        toward(far, True, False)

    @pl.when((1 - early) * inner == 1)
    def _():
        toward(far, True, True)
        toward(across, True, True)

    send_direct(0)
    relay(0)

    for part in range(2):
        line(near, near, part, False).wait_recv()
    send_relayed(1)

    finish_direct(0)
    finish_diagonal(0)

    send_direct(1)
    arrive(1, FROM_X, 0, sx)
    push(1, DIAGONAL, 0, sx, sy)
    push(1, CORE_X, 0, sx, sc)

    @pl.when((1 - early) * (1 - inner) == 1)
    def _():
        toward(across, True, True)
        toward(far, True, True)

    arrive(1, FROM_Y, 1, sy)
    push(1, DIAGONAL, 1, sy, sx)
    push(1, CORE_Y, 1, sy, sc)

    for part in range(2):
        line(third, third, part, False).wait_recv()
        push(2, FROM_X, part, s, sx)
        if part == 0:
            push(2, FROM_Y, part, s, sy)
        push(2, CORE_OWN, part, s, sc)
    finish_direct(1)
    finish_diagonal(1)
    arrive(2, FROM_Y, 0, sy)
    push(2, DIAGONAL, 0, sy, sx)
    push(2, CORE_Y, 0, sy, sc)
    arrive(2, FROM_X, 0, sx, theirs)
    push(2, CORE_X, 0, sx, sc, theirs)
    for q in QUARTERS:
        line(fourth, fourth, q, True).wait_recv()
        push_strip(STRIP_Y, q, s, sy)
        push_strip(CORE_STRIP, q, s, sc)
    push(2, FROM_Y, 1, s, sy)
    arrive(2, FROM_X, 1, sx, theirs)
    push(2, CORE_X, 1, sx, sc, theirs)
    push(2, DIAGONAL, 1, sx, sy, theirs)
    drain(0)
    multiply(z, every, True)
    from_core(2, CORE_OWN, sc)
    for q in QUARTERS:
        strip_arrived(STRIP_Y, q, sy)
        push_strip(CORE_STRIP_Y, q, sy, sc)
        strip_arrived(CORE_STRIP, q, sc)
        strip_arrived(CORE_STRIP_Y, q, twin(sy))
        encode(q)
        if q == 0:
            drain(1)
            multiply(near, mine, True)
        elif q == 1:
            multiply(near, [sx // 2, sd // 2], False)
            from_core(2, CORE_X, twin(sx), theirs)
    arrive(2, FROM_Y, 1, sy)
    push(2, CORE_Y, 1, sy, sc)
    from_core(2, CORE_Y, twin(sy))
    multiply(third, mine, True)
    multiply(fourth, mine + [sx // 2], True)
    finish_diagonal(2, theirs)
    for q in range(3):
        decode(q)
    from_core(2, CORE_DIAGONAL, twin(sd), theirs)
    multiply(fourth, [sd // 2], False)
    decode(3)

    for args in started:
        args.wait_send()
    for q in QUARTERS:
        sums_copy(q).wait_send()
    toward(near, False, False)

    @pl.when(early == 1)
    def _():
        toward(across, False, False)
        toward(far, False, False)

    @pl.when(early == 0)
    def _():
        toward(across, False, True)
        toward(far, False, True)


def in_one_kernel(spectra):
    freqs, parts, rows, cols = spectra.shape
    full = cols * LINE
    return pl.pallas_call(
        functools.partial(kernel, rows, cols, -1.0 / math.sqrt(full)),
        out_shape=pltpu.VMEM((parts, rows, full), jnp.float32),
        in_specs=[pl.BlockSpec(memory_space=pltpu.HBM)],
        out_specs=pl.BlockSpec(memory_space=pltpu.VMEM),
        scratch_shapes=[
            pltpu.VMEM((parts, LINE, rows * PLANE, cols), jnp.bfloat16),
            pltpu.VMEM((4, parts * rows + 16, cols // 4), jnp.bfloat16),
            pltpu.VMEM((4, parts * rows + 16, cols // 4), jnp.bfloat16),
            pltpu.SemaphoreType.DMA,
            pltpu.SemaphoreType.DMA((LINE, 4)),
            pltpu.SemaphoreType.DMA((LINE, 4)),
            pltpu.SemaphoreType.DMA((LINE, KINDS)),
            pltpu.SemaphoreType.DMA((LINE, KINDS)),
        ],
        compiler_params=pltpu.CompilerParams(
            collective_id=0, has_side_effects=True, vmem_limit_bytes=28 * 2**20
        ),
    )(pltpu.with_memory_space_constraint(spectra, pltpu.HBM))[None]


def by_collectives(spectra):
    own_rows = lax.all_to_all(spectra, "rcv", split_axis=0, concat_axis=3, tiled=True)
    full = own_rows.shape[3]
    gathered = lax.all_gather(own_rows, "shot", axis=2, tiled=True)
    dot = functools.partial(jnp.einsum, "ang,agv->anv", preferred_element_type=jnp.float32)
    real = dot(own_rows[:, 0], gathered[:, 0]) - dot(own_rows[:, 1], gathered[:, 1])
    imag = dot(own_rows[:, 0], gathered[:, 1]) + dot(own_rows[:, 1], gathered[:, 0])
    return jnp.stack([real, imag], axis=1) * (-1.0 / math.sqrt(full))


def solution(mesh):
    fits = mesh.shape["shot"] == PLANE and mesh.shape["rcv"] == LINE
    return jax.shard_map(
        in_one_kernel if fits else by_collectives,
        mesh=mesh,
        in_specs=(P(None, None, "shot", "rcv"),),
        out_specs=P("rcv", None, "shot", None),
        check_vma=False,
    )
```
